32 devices in a mesh: rows: 8 (over z, y), cols: 4 (over x, core).
Axes of the slice: x: 2, y: 2, z: 4, core: 2. Of those that a mesh axis runs over, the one named last changes fastest.
Arguments:
- vectors: float32 [16384, 512], P('rows', 'cols'), may hold values from -6 to 6
- reflectors: float32 [3, 128, 256, 128], P(None, ('rows', 'cols')), may hold values from -1.05 to 1.05, as said below
- factors: float32 [3, 128, 128, 128], P(None, ('rows', 'cols')), may hold values from -0.25 to 1.1, as said below
- starts: int32 [3, 128], P(None, 'rows'), may hold values from 0 to 16256, as said below
Outputs:
- transformed: float32 [16384, 512], P('rows', 'cols')
The draws below stay inside these ranges and needn't reach their ends.
Inputs may be any that keep to these rules, and one draw needn't show every extreme that they name: `reflectors`: each diamond's matrix is unit lower trapezoidal: entry (i, j) is 1 for i = j and 0 for i < j. `factors`: upper triangular; F is the compact-WY factor of the diamond's reflectors, the inverse of the upper triangle of V^T V with its diagonal halved, so that I - V F V^T is orthogonal. starts[t, g] lies between 128 * g and 128 * g + 64; for the first diamond and for the last diamond of every aligned block of 16 diamonds it equals 128 * g.
All inputs are finite; a program needn't handle non-finite values.
Results may differ from the reference program's by a relative error of at most 0.0003.
Values sent between devices are 32-bit elements; how exact they have to be, the bound alone decides.
A program may use at most 64 MiB of HBM per device.

```python
import jax
import jax.numpy as jnp
from jax import lax

BLOCK = 128
DIA_DEV = 16
TICKS = 3
NR = 16384
NC = 512
NDIA = 128


def householder_panel(key):
    key_lead, key_sign, key_noise = jax.random.split(jax.random.fold_in(key, 37), 3)
    shape = (TICKS, NDIA, 2 * BLOCK, BLOCK)
    spread = 0.05 / BLOCK ** 0.5
    noise = jnp.clip(jax.random.normal(key_noise, shape, jnp.float32), -4.0, 4.0) * spread
    magnitude = jax.random.uniform(key_lead, (TICKS, NDIA, BLOCK), jnp.float32, 0.97, 1.03)
    sign_bits = jax.random.randint(key_sign, (TICKS, NDIA, BLOCK), 0, 2, jnp.int32)
    partner = magnitude * (2 * sign_bits - 1).astype(jnp.float32)
    row_ids = jnp.arange(2 * BLOCK, dtype=jnp.int32)[:, None]
    col_ids = jnp.arange(BLOCK, dtype=jnp.int32)[None, :]
    is_diag = row_ids == col_ids
    is_partner = row_ids == col_ids + BLOCK
    is_below = row_ids > col_ids
    panel = jnp.where(is_below, noise, 0.0)
    panel = jnp.where(is_partner, partner[..., None, :], panel)
    panel = jnp.where(is_diag, 1.0, panel)
    return panel.astype(jnp.float32)


def draw_reflectors(key, part):
    return householder_panel(key)


def draw_factors(key, part):
    panel = householder_panel(key)
    gram = jnp.einsum('tgri,tgrj->tgij', panel, panel, precision=lax.Precision.HIGHEST)
    unit = jnp.eye(BLOCK, dtype=jnp.float32)
    inverse_factor = jnp.triu(gram, 1) + 0.5 * gram * unit
    identity_stack = jnp.broadcast_to(unit, inverse_factor.shape)
    factor = jnp.linalg.solve(inverse_factor, identity_stack)
    return jnp.triu(factor).astype(jnp.float32)


def draw_starts(key, part):
    shift_rows = jax.random.randint(jax.random.fold_in(key, 23), (TICKS, NDIA), 0, BLOCK // 2 + 1, jnp.int32)
    index_rows = jnp.arange(NDIA, dtype=jnp.int32)
    is_fixed = jnp.logical_or(index_rows % DIA_DEV == DIA_DEV - 1, index_rows == 0)
    shift_rows = jnp.where(is_fixed[None, :], 0, shift_rows)
    return (BLOCK * index_rows[None, :] + shift_rows).astype(jnp.int32)


def steps_of(own_key, extent, shards, smallest, top_value):
    def one(dim, parts):
        draws = jax.random.uniform(jax.random.fold_in(jax.random.fold_in(own_key, 6), dim), (parts,), jnp.float32, smallest / len(shards), top_value / len(shards))
        return jnp.repeat(jnp.exp(draws), extent[dim] // parts).reshape((-1,) + (1,) * (len(extent) - dim - 1))

    loudness = one(*shards[0])
    for cut in shards[1:]:
        loudness = loudness * one(*cut)
    return loudness


def bell_draw(rng, shape, width, limit, cuts=(), held_as=jnp.bfloat16):
    gain = steps_of(rng, shape, cuts, -0.22, 0.18) if cuts else 1.0
    result = jax.random.normal(rng, shape, jnp.float32) * width * gain
    return jnp.minimum(jnp.maximum(result, -limit), limit).astype(held_as)


def setup_inputs(seed: int = 0) -> dict:
    streams_of = jax.random.split(jax.random.key(seed), 5)
    vectors = bell_draw(streams_of[0], (NR, NC), 1.0, 6.0, ((0, 8), (1, 4)), jnp.float32)
    reflectors = draw_reflectors(jax.random.fold_in(streams_of[4], 71), 0)
    factors = draw_factors(jax.random.fold_in(streams_of[4], 71), 0)
    starts = draw_starts(jax.random.fold_in(streams_of[4], 71), 0)
    return dict(vectors=vectors, reflectors=reflectors, factors=factors, starts=starts)


highest = lax.Precision.HIGHEST

def apply_diamond(matrix, householder, factor, start_row):
    height = householder.shape[0]
    slab_rows = lax.dynamic_slice_in_dim(matrix, start_row, height, 0)
    projected = jnp.dot(householder.T.astype(jnp.float32), slab_rows.astype(jnp.float32), precision=highest, preferred_element_type=jnp.float32)
    scaled = jnp.dot(factor.astype(jnp.float32), projected.astype(jnp.float32), precision=highest, preferred_element_type=jnp.float32)
    slab_rows = slab_rows - jnp.dot(householder.astype(jnp.float32), scaled.astype(jnp.float32), precision=highest, preferred_element_type=jnp.float32)
    return lax.dynamic_update_slice_in_dim(matrix, slab_rows, start_row, 0)

def reference(vectors, reflectors, factors, starts):
    total_rows = vectors.shape[0]
    col_count = vectors.shape[1]
    diamond_count = starts.shape[1]
    padded = jnp.concatenate([vectors, jnp.zeros((BLOCK, col_count), jnp.float32)], 0)
    for tick_index in range(TICKS):
        tick_refl = reflectors[tick_index]
        tick_fact = factors[tick_index]
        tick_start = starts[tick_index]

        def apply_step(counter, matrix):
            which = diamond_count - 1 - counter
            householder = lax.dynamic_index_in_dim(tick_refl, which, 0, False)
            factor = lax.dynamic_index_in_dim(tick_fact, which, 0, False)
            start_row = lax.dynamic_index_in_dim(tick_start, which, 0, False)
            return apply_diamond(matrix, householder, factor, start_row)
        padded = lax.fori_loop(0, diamond_count, apply_step, padded)
        padded = jnp.concatenate([padded[:total_rows], jnp.zeros((BLOCK, col_count), jnp.float32)], 0)
    return padded[:total_rows]
```

```python
import functools

import jax
import jax.numpy as jnp
from jax import lax
from jax.experimental import pallas as pl
from jax.experimental.pallas import tpu as pltpu
from jax.sharding import PartitionSpec as P

MESH = pl.DeviceIdType.MESH
SHIFT = 64
f32, bf16 = jnp.float32, jnp.bfloat16


def split(x):
    high = x.astype(bf16)
    return high, (x - high.astype(f32)).astype(bf16)


def dot(a, b):
    return jnp.dot(a, b, preferred_element_type=f32)


def product(a, b):
    ah, al = split(a)
    bh, bl = split(b)
    return dot(ah, bh) + (dot(al, bh) + dot(ah, bl))


def kernel(
    n_rows, n_cols,
    vec_ref, pack_ref, start_ref, out_ref,
    gat, work, vstk, wcat, inflow, head, outb, tailb,
    vec_sem, own_sem, g_send, g_recv, p_send, p_recv, f_send, f_recv,
    i_send, i_recv, h_send, h_recv,
):
    row = lax.axis_index("rows")
    col = lax.axis_index("cols")
    ticks, per, height, block = pack_ref.shape
    rows_here, width = vec_ref.shape
    n_dia = per * n_cols
    reach = height + SHIFT
    chips = n_cols // 2
    chip, core = lax.div(col, 2), lax.rem(col, 2)
    partner = chip * 2 + 1 - core
    above, below = lax.rem(row + n_rows - 1, n_rows), lax.rem(row + 1, n_rows)

    def peer_of(j):
        return lax.rem(chip + j, chips) * 2 + core

    def share(tick, owner):
        return gat.at[tick, pl.ds(owner * per, per)]

    vec_copy = pltpu.make_async_copy(
        vec_ref, work.at[pl.ds(0, rows_here), pl.ds(0, width)], vec_sem)
    vec_copy.start()

    def own_copy(tick):
        return pltpu.make_async_copy(pack_ref.at[tick], share(tick, col), own_sem.at[tick])

    barrier = pltpu.get_barrier_semaphore()
    for there in (above, below):
        pl.semaphore_signal(barrier, inc=1, device_id={"rows": there}, device_id_type=MESH)
    for j in range(1, chips):
        pl.semaphore_signal(barrier, inc=1, device_id={"cols": peer_of(j)}, device_id_type=MESH)
    pl.semaphore_signal(barrier, inc=1, device_id={"cols": partner}, device_id_type=MESH)
    pl.semaphore_wait(barrier, 2 + chips)

    def to_peer(tick, j):
        return pltpu.make_async_remote_copy(
            src_ref=pack_ref.at[tick], dst_ref=share(tick, col),
            send_sem=g_send.at[tick, j - 1], recv_sem=g_recv.at[tick, j - 1],
            device_id={"cols": peer_of(j)}, device_id_type=MESH)

    def to_partner(tick):
        return pltpu.make_async_remote_copy(
            src_ref=pack_ref.at[tick], dst_ref=share(tick, col),
            send_sem=p_send.at[tick], recv_sem=p_recv.at[tick],
            device_id={"cols": partner}, device_id_type=MESH)

    def forward(tick, j):
        owner = lax.rem(chip + chips - j, chips) * 2 + core
        return pltpu.make_async_remote_copy(
            src_ref=share(tick, owner), dst_ref=share(tick, owner),
            send_sem=f_send.at[tick, j - 1], recv_sem=f_recv.at[tick, j - 1],
            device_id={"cols": partner}, device_id_type=MESH)

    @pl.loop(0, ticks)
    def _(tick):
        for j in range(1, chips):
            to_peer(tick, j).start()
        to_partner(tick).start()
        own_copy(tick).start()

    def relay(tick):
        for j in range(1, chips):
            to_peer(tick, j).wait_recv()
            forward(tick, j).start()

    ii = lax.broadcasted_iota(jnp.int32, (block, block), 0)
    jj = lax.broadcasted_iota(jnp.int32, (block, block), 1)
    unit = jnp.where(ii == jj, 1.0, 0.0).astype(f32)
    zero = jnp.zeros((block, block), f32)
    total_rows = work.shape[0]
    left, right = pl.ds(0, width), pl.ds(width, block)

    def reset():
        work[pl.ds(rows_here, total_rows - rows_here), :] = jnp.zeros(
            (total_rows - rows_here, width + block), f32)
        work[pl.ds(rows_here, block), right] = unit

    @pl.loop(0, rows_here // block)
    def _(i):
        work[pl.ds(pl.multiple_of(i * block, block), block), right] = zero

    reset()

    def in_block(tick, k):
        return start_ref[tick, k] - row * rows_here - k * block

    def prepare(tick, k, slot):
        top = gat[tick, k, pl.ds(0, block), :]
        lower = jnp.where(ii > jj, top, unit)
        factor = jnp.where(ii <= jj, top, 0.0)
        lower = jnp.where(ii < jj, 0.0, lower)
        house = jnp.concatenate([lower, gat[tick, k, pl.ds(block, height - block), :]], 0)
        pad = jnp.zeros((2 * SHIFT, block), f32)
        house = pltpu.roll(jnp.concatenate([house, pad], 0), in_block(tick, k), 0)
        house = house[:reach]
        high, low = split(house)
        fh, fl = split(factor)
        wide = dot(high, fh) + (dot(low, fh) + dot(high, fl))
        wh, wl = split(wide)
        wcat[slot, :, pl.ds(0, block)] = wh
        wcat[slot, :, pl.ds(block, block)] = wl
        ah, al = split(house.T)
        vstk[slot, pl.ds(0, block), :] = ah
        vstk[slot, pl.ds(block, block), :] = al

    def apply(tick, k, slot):
        base = pl.multiple_of(k * block, block)
        window = pl.ds(base, reach)
        slab = work[window, :]
        vs = vstk[slot]
        wc = wcat[slot]
        sh, sl = split(slab)
        both = dot(vs, sh)
        proj = both[:block] + (both[block:] + dot(vs[:block], sl))
        ph, plow = split(proj)
        delta = dot(wc, jnp.concatenate([ph, ph], 0)) + dot(wc[:, :block], plow)
        work[window, :] = slab - delta

    def send_up(tick):
        return pltpu.make_async_remote_copy(
            src_ref=outb.at[tick], dst_ref=inflow.at[tick],
            send_sem=i_send.at[tick], recv_sem=i_recv.at[tick],
            device_id={"rows": above}, device_id_type=MESH)

    def send_down(tick):
        return pltpu.make_async_remote_copy(
            src_ref=tailb.at[tick], dst_ref=head.at[tick],
            send_sem=h_send.at[tick], recv_sem=h_recv.at[tick],
            device_id={"rows": below}, device_id_type=MESH)

    def take_head(tick):
        send_down(tick).wait_recv()
        work[pl.ds(0, block), left] = head[tick]

    vec_copy.wait()
    relay(0)

    @pl.loop(0, ticks)
    def _(tick):
        own_copy(tick).wait()
        to_partner(tick).wait_recv()
        for j in range(1, chips):
            forward(tick, j).wait_recv()

        prepare(tick, n_dia - 1, lax.rem(n_dia - 1, 2))

        @pl.loop(0, n_dia - 1)
        def _(counter):
            k = n_dia - 1 - counter
            apply(tick, k, lax.rem(k, 2))
            prepare(tick, k - 1, lax.rem(k - 1, 2))

        @pl.when(jnp.logical_and(row > 0, tick > 0))
        def _():
            take_head(tick - 1)

        apply(tick, 0, 0)

        @pl.when(row == n_rows - 1)
        def _():
            outb[tick] = work[pl.ds(0, block), left]
            send_up(tick).start()

        @pl.when(row < n_rows - 1)
        def _():
            send_up(tick).wait_recv()
            flow = inflow[tick]

            @pl.when(row > 0)
            def _():
                outb[tick] = work[pl.ds(0, block), left] + product(
                    work[pl.ds(0, block), right], flow)
                send_up(tick).start()

            tail = pl.ds(rows_here, block)
            tailb[tick] = work[tail, left] + product(work[tail, right], flow)
            send_down(tick).start()
            fh, fl = split(flow)
            fcat = jnp.concatenate([fh, fh], 0)

            @pl.loop(0, rows_here // 256)
            def _(i):
                rows = pl.ds(pl.multiple_of(i * 256, 256), 256)
                rh, rl = split(work[rows, right])
                work[rows, left] = work[rows, left] + (
                    dot(jnp.concatenate([rh, rl], 1), fcat) + dot(rh, fl))

        @pl.when(tick < ticks - 1)
        def _():
            relay(tick + 1)

            @pl.loop(0, rows_here // block)
            def _(i):
                work[pl.ds(pl.multiple_of(i * block, block), block), right] = zero
            reset()

    @pl.when(row > 0)
    def _():
        take_head(ticks - 1)

    out_copy = pltpu.make_async_copy(
        work.at[pl.ds(0, rows_here), pl.ds(0, width)], out_ref, vec_sem)
    out_copy.start()

    @pl.loop(0, ticks)
    def _(tick):
        for j in range(1, chips):
            to_peer(tick, j).wait_send()
            forward(tick, j).wait_send()
        to_partner(tick).wait_send()

        @pl.when(row > 0)
        def _():
            send_up(tick).wait_send()

        @pl.when(row < n_rows - 1)
        def _():
            send_down(tick).wait_send()

    out_copy.wait()


def solution(mesh):
    n_rows, n_cols = mesh.shape["rows"], mesh.shape["cols"]

    def on_device(vectors, reflectors, factors, starts):
        rows_here, width = vectors.shape
        ticks, per, height, block = reflectors.shape
        chips = n_cols // 2
        ii = lax.broadcasted_iota(jnp.int32, factors.shape, 2)
        jj = lax.broadcasted_iota(jnp.int32, factors.shape, 3)
        top = jnp.where(ii > jj, reflectors[:, :, :block], factors)
        packed = jnp.concatenate([top, reflectors[:, :, block:]], 2)
        dma = pltpu.SemaphoreType.DMA
        hops = max(chips - 1, 1)
        reach = height + SHIFT
        edge = (ticks, block, width)
        return pl.pallas_call(
            functools.partial(kernel, n_rows, n_cols),
            out_shape=jax.ShapeDtypeStruct(vectors.shape, f32),
            in_specs=[
                pl.BlockSpec(memory_space=pl.ANY),
                pl.BlockSpec(memory_space=pl.ANY),
                pl.BlockSpec(memory_space=pltpu.SMEM),
            ],
            out_specs=pl.BlockSpec(memory_space=pl.ANY),
            scratch_shapes=[
                pltpu.VMEM((ticks, per * n_cols, height, block), f32),
                pltpu.VMEM((rows_here + height - block + SHIFT, width + block), f32),
                pltpu.VMEM((2, 2 * block, reach), bf16),
                pltpu.VMEM((2, reach, 2 * block), bf16),
                pltpu.VMEM(edge, f32), pltpu.VMEM(edge, f32),
                pltpu.VMEM(edge, f32), pltpu.VMEM(edge, f32),
                dma, dma((ticks,)),
                dma((ticks, hops)), dma((ticks, hops)),
                dma((ticks,)), dma((ticks,)),
                dma((ticks, hops)), dma((ticks, hops)),
                dma((ticks,)), dma((ticks,)), dma((ticks,)), dma((ticks,)),
            ],
            compiler_params=pltpu.CompilerParams(
                collective_id=0, has_side_effects=True, vmem_limit_bytes=40 * 2**20),
        )(vectors, packed, starts)

    return jax.shard_map(
        on_device,
        mesh=mesh,
        in_specs=(
            P("rows", "cols"),
            P(None, ("rows", "cols"), None, None),
            P(None, ("rows", "cols"), None, None),
            P(None, "rows"),
        ),
        out_specs=P("rows", "cols"),
        check_vma=False,
    )
```

```python
import functools

import jax
import jax.numpy as jnp
from jax import lax
from jax.experimental import pallas as pl
from jax.experimental.pallas import tpu as pltpu
from jax.sharding import PartitionSpec as P

MESH = pl.DeviceIdType.MESH
SHIFT = 64
CHUNKS = 4
f32, bf16 = jnp.float32, jnp.bfloat16


def split(x):
    high = x.astype(bf16)
    return high, (x - high.astype(f32)).astype(bf16)


def dot(a, b):
    return jnp.dot(a, b, preferred_element_type=f32)


def product(a, b):
    ah, al = split(a)
    bh, bl = split(b)
    return dot(ah, bh) + (dot(al, bh) + dot(ah, bl))


def kernel(
    n_rows, n_cols,
    vec_ref, pack_ref, start_ref, out_ref,
    gat, work, vhi, vlo, whi, wlo, inflow, head, outb, tailb,
    vec_sem, own_sem, g_send, g_recv, p_send, p_recv, f_send, f_recv,
    i_send, i_recv, h_send, h_recv,
):
    row = lax.axis_index("rows")
    col = lax.axis_index("cols")
    ticks, per, height, block = pack_ref.shape
    rows_here, width = vec_ref.shape
    n_dia = per * n_cols
    reach = height + SHIFT
    pairs, chunk = n_dia // 2, width // CHUNKS
    chips = n_cols // 2
    chip, core = lax.div(col, 2), lax.rem(col, 2)
    partner = chip * 2 + 1 - core
    above, below = lax.rem(row + n_rows - 1, n_rows), lax.rem(row + 1, n_rows)

    def peer_of(j):
        return lax.rem(chip + j, chips) * 2 + core

    def share(tick, owner):
        return gat.at[tick, pl.ds(owner * per, per)]

    vec_copy = pltpu.make_async_copy(
        vec_ref, work.at[pl.ds(0, rows_here), pl.ds(0, width)], vec_sem)
    vec_copy.start()

    def own_copy(tick):
        return pltpu.make_async_copy(pack_ref.at[tick], share(tick, col), own_sem.at[tick])

    barrier = pltpu.get_barrier_semaphore()
    for there in (above, below):
        pl.semaphore_signal(barrier, inc=1, device_id={"rows": there}, device_id_type=MESH)
    for j in range(1, chips):
        pl.semaphore_signal(barrier, inc=1, device_id={"cols": peer_of(j)}, device_id_type=MESH)
    pl.semaphore_signal(barrier, inc=1, device_id={"cols": partner}, device_id_type=MESH)
    pl.semaphore_wait(barrier, 2 + chips)

    def to_peer(tick, j):
        return pltpu.make_async_remote_copy(
            src_ref=pack_ref.at[tick], dst_ref=share(tick, col),
            send_sem=g_send.at[tick, j - 1], recv_sem=g_recv.at[tick, j - 1],
            device_id={"cols": peer_of(j)}, device_id_type=MESH)

    def to_partner(tick):
        return pltpu.make_async_remote_copy(
            src_ref=pack_ref.at[tick], dst_ref=share(tick, col),
            send_sem=p_send.at[tick], recv_sem=p_recv.at[tick],
            device_id={"cols": partner}, device_id_type=MESH)

    def forward(tick, j):
        owner = lax.rem(chip + chips - j, chips) * 2 + core
        return pltpu.make_async_remote_copy(
            src_ref=share(tick, owner), dst_ref=share(tick, owner),
            send_sem=f_send.at[tick, j - 1], recv_sem=f_recv.at[tick, j - 1],
            device_id={"cols": partner}, device_id_type=MESH)

    @pl.loop(0, ticks)
    def _(tick):
        for j in range(1, chips):
            to_peer(tick, j).start()
        to_partner(tick).start()
        own_copy(tick).start()

    def relay(tick):
        for j in range(1, chips):
            to_peer(tick, j).wait_recv()
            forward(tick, j).start()

    ii = lax.broadcasted_iota(jnp.int32, (block, block), 0)
    jj = lax.broadcasted_iota(jnp.int32, (block, block), 1)
    unit = jnp.where(ii == jj, 1.0, 0.0).astype(f32)
    zero = jnp.zeros((block, block), f32)
    total_rows = work.shape[0]
    left, right = pl.ds(0, width), pl.ds(width, block)

    def reset():
        work[pl.ds(rows_here, total_rows - rows_here), :] = jnp.zeros(
            (total_rows - rows_here, width + block), f32)
        work[pl.ds(rows_here, block), right] = unit

    @pl.loop(0, rows_here // block)
    def _(i):
        work[pl.ds(pl.multiple_of(i * block, block), block), right] = zero

    reset()
    for ref in (vhi, vlo, whi, wlo):
        ref[...] = jnp.zeros(ref.shape, bf16)

    def in_block(tick, k):
        return start_ref[tick, k] - row * rows_here - k * block

    def factored(tick, k):
        top = gat[tick, k, pl.ds(0, block), :]
        lower = jnp.where(ii < jj, 0.0, jnp.where(ii > jj, top, unit))
        factor = jnp.where(ii <= jj, top, 0.0)
        house = jnp.concatenate(
            [lower, gat[tick, k, pl.ds(block, height - block), :],
             jnp.zeros((SHIFT, block), f32)], 0)
        house = pltpu.roll(house, in_block(tick, k), 0)
        return house, product(house, factor)

    def prepare(tick, pair, slot):
        va, wa = factored(tick, 2 * pair + 1)
        vb, wb = factored(tick, 2 * pair)
        va, vb = va.T, vb.T
        overlap = reach - block
        cross = product(vb[:, block:], wa[:overlap])
        fix = product(wb, cross)
        first = jnp.concatenate(
            [-fix[:block], wa[:overlap] - fix[block:], wa[overlap:]], 0)
        fh, fl = split(first)
        whi[slot, :, pl.ds(0, block)] = fh
        wlo[slot, :, pl.ds(0, block)] = fl
        sh, sl = split(wb)
        whi[slot, pl.ds(0, reach), pl.ds(block, block)] = sh
        wlo[slot, pl.ds(0, reach), pl.ds(block, block)] = sl
        ah, al = split(va)
        vhi[slot, pl.ds(0, block), pl.ds(block, reach)] = ah
        vlo[slot, pl.ds(0, block), pl.ds(block, reach)] = al
        bh, bl = split(vb)
        vhi[slot, pl.ds(block, block), pl.ds(0, reach)] = bh
        vlo[slot, pl.ds(block, block), pl.ds(0, reach)] = bl

    def apply(pair, slot):
        window = pl.ds(pl.multiple_of(pair * 2 * block, 2 * block), reach + block)
        slab = work[window, :]
        vh, vl, wh, wl = vhi[slot], vlo[slot], whi[slot], wlo[slot]
        sh, sl = split(slab)
        proj = dot(vh, sh) + (dot(vl, sh) + dot(vh, sl))
        ph, plow = split(proj)
        delta = dot(wh, ph) + (dot(wl, ph) + dot(wh, plow))
        work[window, :] = slab - delta

    def send_up(tick, c):
        part = pl.ds(c * chunk, chunk)
        return pltpu.make_async_remote_copy(
            src_ref=outb.at[tick, part], dst_ref=inflow.at[tick, part],
            send_sem=i_send.at[tick, c], recv_sem=i_recv.at[tick, c],
            device_id={"rows": above}, device_id_type=MESH)

    def send_down(tick):
        return pltpu.make_async_remote_copy(
            src_ref=tailb.at[tick], dst_ref=head.at[tick],
            send_sem=h_send.at[tick], recv_sem=h_recv.at[tick],
            device_id={"rows": below}, device_id_type=MESH)

    def take_head(tick):
        send_down(tick).wait_recv()
        work[pl.ds(0, block), left] = head[tick]

    vec_copy.wait()
    relay(0)

    @pl.loop(0, ticks)
    def _(tick):
        own_copy(tick).wait()
        to_partner(tick).wait_recv()
        for j in range(1, chips):
            forward(tick, j).wait_recv()

        prepare(tick, pairs - 1, lax.rem(pairs - 1, 2))

        @pl.loop(0, pairs - 1)
        def _(counter):
            pair = pairs - 1 - counter
            apply(pair, lax.rem(pair, 2))
            prepare(tick, pair - 1, lax.rem(pair - 1, 2))

        @pl.when(jnp.logical_and(row > 0, tick > 0))
        def _():
            take_head(tick - 1)

        apply(0, 0)
        outb[tick] = work[pl.ds(0, block), left].T

        @pl.when(row == n_rows - 1)
        def _():
            for c in range(CHUNKS):
                send_up(tick, c).start()

        @pl.when(row < n_rows - 1)
        def _():
            mh, ml = split(work[pl.ds(0, block), right].T)
            for c in range(CHUNKS):
                send_up(tick, c).wait_recv()

                @pl.when(row > 0)
                def _():
                    part = pl.ds(c * chunk, chunk)
                    xh, xl = split(inflow[tick, part, :])
                    outb[tick, part, :] = outb[tick, part, :] + (
                        dot(xh, mh) + (dot(xl, mh) + dot(xh, ml)))
                    send_up(tick, c).start()

            flow = inflow[tick].T
            tail = pl.ds(rows_here, block)
            tailb[tick] = work[tail, left] + product(work[tail, right], flow)
            send_down(tick).start()
            fh, fl = split(flow)
            fcat = jnp.concatenate([fh, fh], 0)

            @pl.loop(0, rows_here // 256)
            def _(i):
                rows = pl.ds(pl.multiple_of(i * 256, 256), 256)
                rh, rl = split(work[rows, right])
                work[rows, left] = work[rows, left] + (
                    dot(jnp.concatenate([rh, rl], 1), fcat) + dot(rh, fl))

        @pl.when(tick < ticks - 1)
        def _():
            relay(tick + 1)

            @pl.loop(0, rows_here // block)
            def _(i):
                work[pl.ds(pl.multiple_of(i * block, block), block), right] = zero
            reset()

    @pl.when(row > 0)
    def _():
        take_head(ticks - 1)

    out_copy = pltpu.make_async_copy(
        work.at[pl.ds(0, rows_here), pl.ds(0, width)], out_ref, vec_sem)
    out_copy.start()

    @pl.loop(0, ticks)
    def _(tick):
        for j in range(1, chips):
            to_peer(tick, j).wait_send()
            forward(tick, j).wait_send()
        to_partner(tick).wait_send()

        @pl.when(row > 0)
        def _():
            for c in range(CHUNKS):
                send_up(tick, c).wait_send()

        @pl.when(row < n_rows - 1)
        def _():
            send_down(tick).wait_send()

    out_copy.wait()


def solution(mesh):
    n_rows, n_cols = mesh.shape["rows"], mesh.shape["cols"]

    def on_device(vectors, reflectors, factors, starts):
        rows_here, width = vectors.shape
        ticks, per, height, block = reflectors.shape
        chips = n_cols // 2
        ii = lax.broadcasted_iota(jnp.int32, factors.shape, 2)
        jj = lax.broadcasted_iota(jnp.int32, factors.shape, 3)
        top = jnp.where(ii > jj, reflectors[:, :, :block], factors)
        packed = jnp.concatenate([top, reflectors[:, :, block:]], 2)
        dma = pltpu.SemaphoreType.DMA
        hops = max(chips - 1, 1)
        reach = height + SHIFT
        edge, flow = (ticks, block, width), (ticks, width, block)
        return pl.pallas_call(
            functools.partial(kernel, n_rows, n_cols),
            out_shape=jax.ShapeDtypeStruct(vectors.shape, f32),
            in_specs=[
                pl.BlockSpec(memory_space=pl.ANY),
                pl.BlockSpec(memory_space=pl.ANY),
                pl.BlockSpec(memory_space=pltpu.SMEM),
            ],
            out_specs=pl.BlockSpec(memory_space=pl.ANY),
            scratch_shapes=[
                pltpu.VMEM((ticks, per * n_cols, height, block), f32),
                pltpu.VMEM((rows_here + height - block + SHIFT, width + block), f32),
                pltpu.VMEM((2, 2 * block, reach + block), bf16),
                pltpu.VMEM((2, 2 * block, reach + block), bf16),
                pltpu.VMEM((2, reach + block, 2 * block), bf16),
                pltpu.VMEM((2, reach + block, 2 * block), bf16),
                pltpu.VMEM(flow, f32), pltpu.VMEM(edge, f32),
                pltpu.VMEM(flow, f32), pltpu.VMEM(edge, f32),
                dma, dma((ticks,)),
                dma((ticks, hops)), dma((ticks, hops)),
                dma((ticks,)), dma((ticks,)),
                dma((ticks, hops)), dma((ticks, hops)),
                dma((ticks, CHUNKS)), dma((ticks, CHUNKS)), dma((ticks,)), dma((ticks,)),
            ],
            compiler_params=pltpu.CompilerParams(
                collective_id=0, has_side_effects=True, vmem_limit_bytes=60 * 2**20),
        )(vectors, packed, starts)

    return jax.shard_map(
        on_device,
        mesh=mesh,
        in_specs=(
            P("rows", "cols"),
            P(None, ("rows", "cols"), None, None),
            P(None, ("rows", "cols"), None, None),
            P(None, "rows"),
        ),
        out_specs=P("rows", "cols"),
        check_vma=False,
    )
```

```python
import functools

import jax
import jax.numpy as jnp
from jax import lax
from jax.experimental import pallas as pl
from jax.experimental.pallas import tpu as pltpu
from jax.sharding import PartitionSpec as P

MESH = pl.DeviceIdType.MESH
SHIFT = 64
CHUNKS = 4
f32, bf16 = jnp.float32, jnp.bfloat16


def split(x):
    high = x.astype(bf16)
    return high, (x - high.astype(f32)).astype(bf16)


def dot(a, b):
    return jnp.dot(a, b, preferred_element_type=f32)


def product(a, b):
    ah, al = split(a)
    bh, bl = split(b)
    return dot(ah, bh) + (dot(al, bh) + dot(ah, bl))


def kernel(
    n_rows, n_cols,
    vec_ref, pack_ref, start_ref, out_ref,
    gat, work, vhi, vlo, wcat, inflow, head, outb, tailb,
    vec_sem, own_sem, g_send, g_recv, p_send, p_recv, f_send, f_recv,
    i_send, i_recv, h_send, h_recv,
):
    row = lax.axis_index("rows")
    col = lax.axis_index("cols")
    ticks, per, height, block = pack_ref.shape
    rows_here, width = vec_ref.shape
    n_dia = per * n_cols
    reach = height + SHIFT
    chunk = width // CHUNKS
    chips = n_cols // 2
    chip, core = lax.div(col, 2), lax.rem(col, 2)
    partner = chip * 2 + 1 - core
    above, below = lax.rem(row + n_rows - 1, n_rows), lax.rem(row + 1, n_rows)

    def peer_of(j):
        return lax.rem(chip + j, chips) * 2 + core

    def share(tick, owner):
        return gat.at[tick, pl.ds(owner * per, per)]

    vec_copy = pltpu.make_async_copy(
        vec_ref, work.at[pl.ds(0, rows_here), pl.ds(0, width)], vec_sem)
    vec_copy.start()

    def own_copy(tick):
        return pltpu.make_async_copy(pack_ref.at[tick], share(tick, col), own_sem.at[tick])

    barrier = pltpu.get_barrier_semaphore()
    for there in (above, below):
        pl.semaphore_signal(barrier, inc=1, device_id={"rows": there}, device_id_type=MESH)
    for j in range(1, chips):
        pl.semaphore_signal(barrier, inc=1, device_id={"cols": peer_of(j)}, device_id_type=MESH)
    pl.semaphore_signal(barrier, inc=1, device_id={"cols": partner}, device_id_type=MESH)
    pl.semaphore_wait(barrier, 2 + chips)

    def to_peer(tick, j):
        return pltpu.make_async_remote_copy(
            src_ref=pack_ref.at[tick], dst_ref=share(tick, col),
            send_sem=g_send.at[tick, j - 1], recv_sem=g_recv.at[tick, j - 1],
            device_id={"cols": peer_of(j)}, device_id_type=MESH)

    def to_partner(tick):
        return pltpu.make_async_remote_copy(
            src_ref=pack_ref.at[tick], dst_ref=share(tick, col),
            send_sem=p_send.at[tick], recv_sem=p_recv.at[tick],
            device_id={"cols": partner}, device_id_type=MESH)

    def forward(tick, j):
        owner = lax.rem(chip + chips - j, chips) * 2 + core
        return pltpu.make_async_remote_copy(
            src_ref=share(tick, owner), dst_ref=share(tick, owner),
            send_sem=f_send.at[tick, j - 1], recv_sem=f_recv.at[tick, j - 1],
            device_id={"cols": partner}, device_id_type=MESH)

    @pl.loop(0, ticks)
    def _(tick):
        for j in range(1, chips):
            to_peer(tick, j).start()
        to_partner(tick).start()
        own_copy(tick).start()

    def relay(tick):
        for j in range(1, chips):
            to_peer(tick, j).wait_recv()
            forward(tick, j).start()

    ii = lax.broadcasted_iota(jnp.int32, (block, block), 0)
    jj = lax.broadcasted_iota(jnp.int32, (block, block), 1)
    unit = jnp.where(ii == jj, 1.0, 0.0).astype(f32)
    zero = jnp.zeros((block, block), f32)
    total_rows = work.shape[0]
    left, right = pl.ds(0, width), pl.ds(width, block)

    def reset():
        work[pl.ds(rows_here, total_rows - rows_here), :] = jnp.zeros(
            (total_rows - rows_here, width + block), f32)
        work[pl.ds(rows_here, block), right] = unit

    @pl.loop(0, rows_here // block)
    def _(i):
        work[pl.ds(pl.multiple_of(i * block, block), block), right] = zero

    reset()

    def in_block(tick, k):
        return start_ref[tick, k] - row * rows_here - k * block

    def prepare(tick, k):
        slot = tick * n_dia + k
        top = gat[tick, k, pl.ds(0, block), :]
        lower = jnp.where(ii < jj, 0.0, jnp.where(ii > jj, top, unit))
        fh, fl = split(jnp.where(ii <= jj, top, 0.0))
        house = jnp.concatenate(
            [lower, gat[tick, k, pl.ds(block, height - block), :],
             jnp.zeros((SHIFT, block), f32)], 0)
        house = pltpu.roll(house, in_block(tick, k), 0)
        high, low = split(house)
        wide = dot(jnp.concatenate([high, low], 1), jnp.concatenate([fh, fh], 0))
        wh, wl = split(wide + dot(high, fl))
        wcat[slot, :, pl.ds(0, block)] = wh
        wcat[slot, :, pl.ds(block, block)] = wl
        ah, al = split(house.T)
        vhi[slot] = ah
        vlo[slot] = al

    def prepare_share(tick, owner):
        @pl.loop(0, per, unroll=min(per, 2))
        def _(i):
            prepare(tick, owner * per + i)

    def apply(tick, k):
        slot = tick * n_dia + k
        window = pl.ds(pl.multiple_of(k * block, block), reach)
        vh, vl, wc = vhi[slot], vlo[slot], wcat[slot]
        slab = work[window, :]
        sh, sl = split(slab)
        hb = block // 2
        proj = jnp.concatenate([
            dot(vh[p:p + hb], sh) + (dot(vl[p:p + hb], sh) + dot(vh[p:p + hb], sl))
            for p in (0, hb)], 0)
        ph, plow = split(proj)
        pp = jnp.concatenate([ph, ph], 0)
        hr = reach // 2
        for p in (0, hr):
            part = wc[p:p + hr]
            delta = dot(part, pp) + dot(part[:, :block], plow)
            work[pl.ds(pl.multiple_of(k * block, block) + p, hr), :] = slab[p:p + hr] - delta

    def send_up(tick, c):
        part = pl.ds(c * chunk, chunk)
        return pltpu.make_async_remote_copy(
            src_ref=outb.at[tick, part], dst_ref=inflow.at[tick, part],
            send_sem=i_send.at[tick, c], recv_sem=i_recv.at[tick, c],
            device_id={"rows": above}, device_id_type=MESH)

    def send_down(tick):
        return pltpu.make_async_remote_copy(
            src_ref=tailb.at[tick], dst_ref=head.at[tick],
            send_sem=h_send.at[tick], recv_sem=h_recv.at[tick],
            device_id={"rows": below}, device_id_type=MESH)

    def take_head(tick):
        send_down(tick).wait_recv()
        work[pl.ds(0, block), left] = head[tick]

    @pl.loop(0, 2 * ticks)
    def _(m):
        mine = m < ticks
        tick = jnp.where(mine, m, m - ticks)

        @pl.when(mine)
        def _():
            own_copy(tick).wait()

        @pl.when(jnp.logical_not(mine))
        def _():
            to_partner(tick).wait_recv()

        prepare_share(tick, jnp.where(mine, col, partner))

    vec_copy.wait()
    relay(0)

    @pl.loop(0, ticks)
    def _(tick):
        @pl.loop(0, 2 * (chips - 1))
        def _(m):
            far = m >= chips - 1
            j = jnp.where(far, m - (chips - 1), m) + 1

            @pl.when(far)
            def _():
                forward(tick, j).wait_recv()

            owner = lax.rem(chip + chips - j, chips) * 2
            prepare_share(tick, owner + jnp.where(far, 1 - core, core))

        @pl.loop(0, n_dia - 1)
        def _(counter):
            k = n_dia - 1 - counter
            apply(tick, k)

        @pl.when(jnp.logical_and(row > 0, tick > 0))
        def _():
            take_head(tick - 1)

        apply(tick, 0)
        outb[tick] = work[pl.ds(0, block), left].T

        @pl.when(row == n_rows - 1)
        def _():
            for c in range(CHUNKS):
                send_up(tick, c).start()

        @pl.when(row < n_rows - 1)
        def _():
            mh, ml = split(work[pl.ds(0, block), right].T)
            for c in range(CHUNKS):
                send_up(tick, c).wait_recv()

                @pl.when(row > 0)
                def _():
                    part = pl.ds(c * chunk, chunk)
                    xh, xl = split(inflow[tick, part, :])
                    outb[tick, part, :] = outb[tick, part, :] + (
                        dot(xh, mh) + (dot(xl, mh) + dot(xh, ml)))
                    send_up(tick, c).start()

            flow = inflow[tick].T
            tail = pl.ds(rows_here, block)
            tailb[tick] = work[tail, left] + product(work[tail, right], flow)
            send_down(tick).start()
            fh, fl = split(flow)
            fcat = jnp.concatenate([fh, fh], 0)

            @pl.loop(0, rows_here // 256)
            def _(i):
                rows = pl.ds(pl.multiple_of(i * 256, 256), 256)
                rh, rl = split(work[rows, right])
                work[rows, left] = work[rows, left] + (
                    dot(jnp.concatenate([rh, rl], 1), fcat) + dot(rh, fl))

        @pl.when(tick < ticks - 1)
        def _():
            relay(tick + 1)

            @pl.loop(0, rows_here // block)
            def _(i):
                work[pl.ds(pl.multiple_of(i * block, block), block), right] = zero
            reset()

    @pl.when(row > 0)
    def _():
        take_head(ticks - 1)

    out_copy = pltpu.make_async_copy(
        work.at[pl.ds(0, rows_here), pl.ds(0, width)], out_ref, vec_sem)
    out_copy.start()

    @pl.loop(0, ticks)
    def _(tick):
        for j in range(1, chips):
            to_peer(tick, j).wait_send()
            forward(tick, j).wait_send()
        to_partner(tick).wait_send()

        @pl.when(row > 0)
        def _():
            for c in range(CHUNKS):
                send_up(tick, c).wait_send()

        @pl.when(row < n_rows - 1)
        def _():
            send_down(tick).wait_send()

    out_copy.wait()


def solution(mesh):
    n_rows, n_cols = mesh.shape["rows"], mesh.shape["cols"]

    def on_device(vectors, reflectors, factors, starts):
        rows_here, width = vectors.shape
        ticks, per, height, block = reflectors.shape
        chips = n_cols // 2
        ii = lax.broadcasted_iota(jnp.int32, factors.shape, 2)
        jj = lax.broadcasted_iota(jnp.int32, factors.shape, 3)
        top = jnp.where(ii > jj, reflectors[:, :, :block], factors)
        packed = jnp.concatenate([top, reflectors[:, :, block:]], 2)
        dma = pltpu.SemaphoreType.DMA
        hops = max(chips - 1, 1)
        reach = height + SHIFT
        edge, flow = (ticks, block, width), (ticks, width, block)
        return pl.pallas_call(
            functools.partial(kernel, n_rows, n_cols),
            out_shape=jax.ShapeDtypeStruct(vectors.shape, f32),
            in_specs=[
                pl.BlockSpec(memory_space=pl.ANY),
                pl.BlockSpec(memory_space=pl.ANY),
                pl.BlockSpec(memory_space=pltpu.SMEM),
            ],
            out_specs=pl.BlockSpec(memory_space=pl.ANY),
            scratch_shapes=[
                pltpu.VMEM((ticks, per * n_cols, height, block), f32),
                pltpu.VMEM((rows_here + height - block + SHIFT, width + block), f32),
                pltpu.VMEM((ticks * per * n_cols, block, reach), bf16),
                pltpu.VMEM((ticks * per * n_cols, block, reach), bf16),
                pltpu.VMEM((ticks * per * n_cols, reach, 2 * block), bf16),
                pltpu.VMEM(flow, f32), pltpu.VMEM(edge, f32),
                pltpu.VMEM(flow, f32), pltpu.VMEM(edge, f32),
                dma, dma((ticks,)),
                dma((ticks, hops)), dma((ticks, hops)),
                dma((ticks,)), dma((ticks,)),
                dma((ticks, hops)), dma((ticks, hops)),
                dma((ticks, CHUNKS)), dma((ticks, CHUNKS)), dma((ticks,)), dma((ticks,)),
            ],
            compiler_params=pltpu.CompilerParams(
                collective_id=0, has_side_effects=True, vmem_limit_bytes=60 * 2**20),
        )(vectors, packed, starts)

    return jax.shard_map(
        on_device,
        mesh=mesh,
        in_specs=(
            P("rows", "cols"),
            P(None, ("rows", "cols"), None, None),
            P(None, ("rows", "cols"), None, None),
            P(None, "rows"),
        ),
        out_specs=P("rows", "cols"),
        check_vma=False,
    )
```

```python
import functools

import jax
import jax.numpy as jnp
from jax import lax
from jax.experimental import pallas as pl
from jax.experimental.pallas import tpu as pltpu
from jax.sharding import PartitionSpec as P

MESH = pl.DeviceIdType.MESH
SHIFT = 64
CHUNKS = 4
f32, bf16 = jnp.float32, jnp.bfloat16


def split(x):
    high = x.astype(bf16)
    return high, (x - high.astype(f32)).astype(bf16)


def dot(a, b):
    return jnp.dot(a, b, preferred_element_type=f32)


def product(a, b):
    ah, al = split(a)
    bh, bl = split(b)
    return dot(ah, bh) + (dot(al, bh) + dot(ah, bl))


def kernel(
    n_rows, n_cols,
    vec_ref, pack_ref, start_ref, out_ref,
    gat, work, vhi, vlo, wcat, inflow, head, outb, tailb,
    vec_sem, own_sem, g_send, g_recv, p_send, p_recv, f_send, f_recv,
    i_send, i_recv, h_send, h_recv,
):
    row = lax.axis_index("rows")
    col = lax.axis_index("cols")
    ticks, per, height, block = pack_ref.shape
    rows_here, width = vec_ref.shape
    n_dia = per * n_cols
    reach = height + SHIFT
    chunk = width // CHUNKS
    chips = n_cols // 2
    chip, core = lax.div(col, 2), lax.rem(col, 2)
    partner = chip * 2 + 1 - core
    above, below = lax.rem(row + n_rows - 1, n_rows), lax.rem(row + 1, n_rows)

    def peer_of(j):
        return lax.rem(chip + j, chips) * 2 + core

    def share(tick, owner):
        return gat.at[tick, pl.ds(owner * per, per)]

    vec_copy = pltpu.make_async_copy(
        vec_ref, work.at[pl.ds(0, rows_here), pl.ds(0, width)], vec_sem)
    vec_copy.start()

    def own_copy(tick):
        return pltpu.make_async_copy(pack_ref.at[tick], share(tick, col), own_sem.at[tick])

    barrier = pltpu.get_barrier_semaphore()
    for there in (above, below):
        pl.semaphore_signal(barrier, inc=1, device_id={"rows": there}, device_id_type=MESH)
    for j in range(1, chips):
        pl.semaphore_signal(barrier, inc=1, device_id={"cols": peer_of(j)}, device_id_type=MESH)
    pl.semaphore_signal(barrier, inc=1, device_id={"cols": partner}, device_id_type=MESH)
    pl.semaphore_wait(barrier, 2 + chips)

    def to_peer(tick, j, i):
        return pltpu.make_async_remote_copy(
            src_ref=pack_ref.at[tick, i], dst_ref=gat.at[tick, col * per + i],
            send_sem=g_send.at[tick, j - 1, i], recv_sem=g_recv.at[tick, j - 1, i],
            device_id={"cols": peer_of(j)}, device_id_type=MESH)

    def to_partner(tick):
        return pltpu.make_async_remote_copy(
            src_ref=pack_ref.at[tick], dst_ref=share(tick, col),
            send_sem=p_send.at[tick], recv_sem=p_recv.at[tick],
            device_id={"cols": partner}, device_id_type=MESH)

    def forward(tick, j, i):
        owner = lax.rem(chip + chips - j, chips) * 2 + core
        return pltpu.make_async_remote_copy(
            src_ref=gat.at[tick, owner * per + i], dst_ref=gat.at[tick, owner * per + i],
            send_sem=f_send.at[tick, j - 1, i], recv_sem=f_recv.at[tick, j - 1, i],
            device_id={"cols": partner}, device_id_type=MESH)

    @pl.loop(0, ticks)
    def _(tick):
        @pl.loop(0, per)
        def _(m):
            for j in range(1, chips):
                to_peer(tick, j, per - 1 - m).start()
        to_partner(tick).start()
        own_copy(tick).start()

    ii = lax.broadcasted_iota(jnp.int32, (block, block), 0)
    jj = lax.broadcasted_iota(jnp.int32, (block, block), 1)
    unit = jnp.where(ii == jj, 1.0, 0.0).astype(f32)
    zero = jnp.zeros((block, block), f32)
    total_rows = work.shape[0]
    left, right = pl.ds(0, width), pl.ds(width, block)

    def reset():
        work[pl.ds(rows_here, total_rows - rows_here), :] = jnp.zeros(
            (total_rows - rows_here, width + block), f32)
        work[pl.ds(rows_here, block), right] = unit

    @pl.loop(0, rows_here // block)
    def _(i):
        work[pl.ds(pl.multiple_of(i * block, block), block), right] = zero

    reset()

    def in_block(tick, k):
        return start_ref[tick, k] - row * rows_here - k * block

    def prepare(tick, k):
        slot = tick * n_dia + k
        top = gat[tick, k, pl.ds(0, block), :]
        lower = jnp.where(ii < jj, 0.0, jnp.where(ii > jj, top, unit))
        fh, fl = split(jnp.where(ii <= jj, top, 0.0))
        house = jnp.concatenate(
            [lower, gat[tick, k, pl.ds(block, height - block), :],
             jnp.zeros((SHIFT, block), f32)], 0)
        house = pltpu.roll(house, in_block(tick, k), 0)
        high, low = split(house)
        wide = dot(jnp.concatenate([high, low], 1), jnp.concatenate([fh, fh], 0))
        wh, wl = split(wide + dot(high, fl))
        wcat[slot, :, pl.ds(0, block)] = wh
        wcat[slot, :, pl.ds(block, block)] = wl
        ah, al = split(house.T)
        vhi[slot] = ah
        vlo[slot] = al

    def prepare_share(tick, owner):
        @pl.loop(0, per, unroll=1)
        def _(i):
            prepare(tick, owner * per + i)

    def apply(tick, k):
        slot = tick * n_dia + k
        window = pl.ds(pl.multiple_of(k * block, block), reach)
        vh, vl, wc = vhi[slot], vlo[slot], wcat[slot]
        slab = work[window, :]
        sh, sl = split(slab)
        hb = block // 2
        proj = jnp.concatenate([
            dot(vh[p:p + hb], sh) + (dot(vl[p:p + hb], sh) + dot(vh[p:p + hb], sl))
            for p in (0, hb)], 0)
        ph, plow = split(proj)
        pp = jnp.concatenate([ph, ph], 0)
        hr = reach // 2
        for p in (0, hr):
            part = wc[p:p + hr]
            delta = dot(part, pp) + dot(part[:, :block], plow)
            work[pl.ds(pl.multiple_of(k * block, block) + p, hr), :] = slab[p:p + hr] - delta

    def send_up(tick, c):
        part = pl.ds(c * chunk, chunk)
        return pltpu.make_async_remote_copy(
            src_ref=outb.at[tick, part], dst_ref=inflow.at[tick, part],
            send_sem=i_send.at[tick, c], recv_sem=i_recv.at[tick, c],
            device_id={"rows": above}, device_id_type=MESH)

    def send_down(tick):
        return pltpu.make_async_remote_copy(
            src_ref=tailb.at[tick], dst_ref=head.at[tick],
            send_sem=h_send.at[tick], recv_sem=h_recv.at[tick],
            device_id={"rows": below}, device_id_type=MESH)

    def take_head(tick):
        send_down(tick).wait_recv()
        work[pl.ds(0, block), left] = head[tick]

    @pl.loop(0, 2 * ticks)
    def _(m):
        mine = m < ticks
        tick = jnp.where(mine, m, m - ticks)

        @pl.when(mine)
        def _():
            own_copy(tick).wait()

        @pl.when(jnp.logical_not(mine))
        def _():
            to_partner(tick).wait_recv()

        prepare_share(tick, jnp.where(mine, col, partner))

    vec_copy.wait()

    @pl.loop(0, ticks)
    def _(tick):
        @pl.loop(0, n_dia)
        def _(counter):
            k = n_dia - 1 - counter
            owner, i = lax.div(k, per), lax.rem(k, per)
            o_chip, o_core = lax.div(owner, 2), lax.rem(owner, 2)
            j = lax.rem(chip + chips - o_chip, chips)

            @pl.when(j > 0)
            def _():
                @pl.when(o_core == 1)
                def _():
                    to_peer(tick, j, i).wait_recv()
                    forward(tick, j, i).start()

                @pl.when(o_core != core)
                def _():
                    forward(tick, j, i).wait_recv()

                prepare(tick, k)

            @pl.when(jnp.logical_and(k == 0, jnp.logical_and(row > 0, tick > 0)))
            def _():
                take_head(jnp.maximum(tick - 1, 0))

            apply(tick, k)

        outb[tick] = work[pl.ds(0, block), left].T

        @pl.when(row == n_rows - 1)
        def _():
            for c in range(CHUNKS):
                send_up(tick, c).start()

        @pl.when(row < n_rows - 1)
        def _():
            mh, ml = split(work[pl.ds(0, block), right].T)
            for c in range(CHUNKS):
                send_up(tick, c).wait_recv()

                @pl.when(row > 0)
                def _():
                    part = pl.ds(c * chunk, chunk)
                    xh, xl = split(inflow[tick, part, :])
                    outb[tick, part, :] = outb[tick, part, :] + (
                        dot(xh, mh) + (dot(xl, mh) + dot(xh, ml)))
                    send_up(tick, c).start()

            flow = inflow[tick].T
            tail = pl.ds(rows_here, block)
            tailb[tick] = work[tail, left] + product(work[tail, right], flow)
            send_down(tick).start()
            fh, fl = split(flow)
            fcat = jnp.concatenate([fh, fh], 0)

            @pl.loop(0, rows_here // 256)
            def _(i):
                rows = pl.ds(pl.multiple_of(i * 256, 256), 256)
                rh, rl = split(work[rows, right])
                work[rows, left] = work[rows, left] + (
                    dot(jnp.concatenate([rh, rl], 1), fcat) + dot(rh, fl))

        @pl.when(tick < ticks - 1)
        def _():
            @pl.loop(0, rows_here // block)
            def _(i):
                work[pl.ds(pl.multiple_of(i * block, block), block), right] = zero
            reset()

    @pl.when(row > 0)
    def _():
        take_head(ticks - 1)

    out_copy = pltpu.make_async_copy(
        work.at[pl.ds(0, rows_here), pl.ds(0, width)], out_ref, vec_sem)
    out_copy.start()

    @pl.loop(0, ticks)
    def _(tick):
        @pl.loop(0, per)
        def _(i):
            for j in range(1, chips):
                to_peer(tick, j, i).wait_send()
                forward(tick, j, i).wait_send()
        to_partner(tick).wait_send()

        @pl.when(row > 0)
        def _():
            for c in range(CHUNKS):
                send_up(tick, c).wait_send()

        @pl.when(row < n_rows - 1)
        def _():
            send_down(tick).wait_send()

    out_copy.wait()


def solution(mesh):
    n_rows, n_cols = mesh.shape["rows"], mesh.shape["cols"]

    def on_device(vectors, reflectors, factors, starts):
        rows_here, width = vectors.shape
        ticks, per, height, block = reflectors.shape
        chips = n_cols // 2
        ii = lax.broadcasted_iota(jnp.int32, factors.shape, 2)
        jj = lax.broadcasted_iota(jnp.int32, factors.shape, 3)
        top = jnp.where(ii > jj, reflectors[:, :, :block], factors)
        packed = jnp.concatenate([top, reflectors[:, :, block:]], 2)
        dma = pltpu.SemaphoreType.DMA
        hops = max(chips - 1, 1)
        reach = height + SHIFT
        edge, flow = (ticks, block, width), (ticks, width, block)
        return pl.pallas_call(
            functools.partial(kernel, n_rows, n_cols),
            out_shape=jax.ShapeDtypeStruct(vectors.shape, f32),
            in_specs=[
                pl.BlockSpec(memory_space=pl.ANY),
                pl.BlockSpec(memory_space=pl.ANY),
                pl.BlockSpec(memory_space=pltpu.SMEM),
            ],
            out_specs=pl.BlockSpec(memory_space=pl.ANY),
            scratch_shapes=[
                pltpu.VMEM((ticks, per * n_cols, height, block), f32),
                pltpu.VMEM((rows_here + height - block + SHIFT, width + block), f32),
                pltpu.VMEM((ticks * per * n_cols, block, reach), bf16),
                pltpu.VMEM((ticks * per * n_cols, block, reach), bf16),
                pltpu.VMEM((ticks * per * n_cols, reach, 2 * block), bf16),
                pltpu.VMEM(flow, f32), pltpu.VMEM(edge, f32),
                pltpu.VMEM(flow, f32), pltpu.VMEM(edge, f32),
                dma, dma((ticks,)),
                dma((ticks, hops, per)), dma((ticks, hops, per)),
                dma((ticks,)), dma((ticks,)),
                dma((ticks, hops, per)), dma((ticks, hops, per)),
                dma((ticks, CHUNKS)), dma((ticks, CHUNKS)), dma((ticks,)), dma((ticks,)),
            ],
            compiler_params=pltpu.CompilerParams(
                collective_id=0, has_side_effects=True, vmem_limit_bytes=36 * 2**20),
        )(vectors, packed, starts)

    return jax.shard_map(
        on_device,
        mesh=mesh,
        in_specs=(
            P("rows", "cols"),
            P(None, ("rows", "cols"), None, None),
            P(None, ("rows", "cols"), None, None),
            P(None, "rows"),
        ),
        out_specs=P("rows", "cols"),
        check_vma=False,
    )
```

```python
import functools

import jax
import jax.numpy as jnp
from jax import lax
from jax.experimental import pallas as pl
from jax.experimental.pallas import tpu as pltpu
from jax.sharding import PartitionSpec as P

MESH = pl.DeviceIdType.MESH
SHIFT = 64
CHUNKS = 4
f32, bf16 = jnp.float32, jnp.bfloat16


def split(x):
    high = x.astype(bf16)
    return high, (x - high.astype(f32)).astype(bf16)


def dot(a, b):
    return jnp.dot(a, b, preferred_element_type=f32)


def product(a, b):
    ah, al = split(a)
    bh, bl = split(b)
    return dot(ah, bh) + (dot(al, bh) + dot(ah, bl))


def kernel(
    n_rows, n_cols,
    vec_ref, pack_ref, start_ref, out_ref,
    gat, work, vhi, vlo, wcat, inflow, head, outb, tailb,
    vec_sem, own_sem, g_send, g_recv, p_send, p_recv, f_send, f_recv,
    i_send, i_recv, h_send, h_recv,
):
    row = lax.axis_index("rows")
    col = lax.axis_index("cols")
    ticks, per, height, block = pack_ref.shape
    rows_here, width = vec_ref.shape
    n_dia = per * n_cols
    reach = height + SHIFT
    chunk = width // CHUNKS
    chips = n_cols // 2
    chip, core = lax.div(col, 2), lax.rem(col, 2)
    partner = chip * 2 + 1 - core
    above, below = lax.rem(row + n_rows - 1, n_rows), lax.rem(row + 1, n_rows)

    def peer_of(j):
        return lax.rem(chip + j, chips) * 2 + core

    def share(tick, owner):
        return gat.at[tick, pl.ds(owner * per, per)]

    vec_copy = pltpu.make_async_copy(
        vec_ref, work.at[pl.ds(0, rows_here), pl.ds(0, width)], vec_sem)
    vec_copy.start()

    def own_copy(tick):
        return pltpu.make_async_copy(pack_ref.at[tick], share(tick, col), own_sem.at[tick])

    barrier = pltpu.get_barrier_semaphore()
    for there in (above, below):
        pl.semaphore_signal(barrier, inc=1, device_id={"rows": there}, device_id_type=MESH)
    for j in range(1, chips):
        pl.semaphore_signal(barrier, inc=1, device_id={"cols": peer_of(j)}, device_id_type=MESH)
    pl.semaphore_signal(barrier, inc=1, device_id={"cols": partner}, device_id_type=MESH)
    pl.semaphore_wait(barrier, 2 + chips)

    def to_peer(tick, j, i):
        return pltpu.make_async_remote_copy(
            src_ref=pack_ref.at[tick, i], dst_ref=gat.at[tick, col * per + i],
            send_sem=g_send.at[tick, j - 1, i], recv_sem=g_recv.at[tick, j - 1, i],
            device_id={"cols": peer_of(j)}, device_id_type=MESH)

    def to_partner(tick):
        return pltpu.make_async_remote_copy(
            src_ref=pack_ref.at[tick], dst_ref=share(tick, col),
            send_sem=p_send.at[tick], recv_sem=p_recv.at[tick],
            device_id={"cols": partner}, device_id_type=MESH)

    def forward(tick, j, i):
        owner = lax.rem(chip + chips - j, chips) * 2 + core
        return pltpu.make_async_remote_copy(
            src_ref=gat.at[tick, owner * per + i], dst_ref=gat.at[tick, owner * per + i],
            send_sem=f_send.at[tick, j - 1, i], recv_sem=f_recv.at[tick, j - 1, i],
            device_id={"cols": partner}, device_id_type=MESH)

    @pl.loop(0, ticks)
    def _(tick):
        @pl.loop(0, per)
        def _(m):
            for j in range(1, chips):
                to_peer(tick, j, per - 1 - m).start()
        to_partner(tick).start()
        own_copy(tick).start()

    ii = lax.broadcasted_iota(jnp.int32, (block, block), 0)
    jj = lax.broadcasted_iota(jnp.int32, (block, block), 1)
    unit = jnp.where(ii == jj, 1.0, 0.0).astype(f32)
    zero = jnp.zeros((block, block), f32)
    total_rows = work.shape[0]
    left, right = pl.ds(0, width), pl.ds(width, block)

    def reset():
        work[pl.ds(rows_here, total_rows - rows_here), :] = jnp.zeros(
            (total_rows - rows_here, width + block), f32)
        work[pl.ds(rows_here, block), right] = unit

    @pl.loop(0, rows_here // block)
    def _(i):
        work[pl.ds(pl.multiple_of(i * block, block), block), right] = zero

    reset()

    def in_block(tick, k):
        return start_ref[tick, k] - row * rows_here - k * block

    def prepare(tick, k):
        slot = tick * n_dia + k
        top = gat[tick, k, pl.ds(0, block), :]
        lower = jnp.where(ii < jj, 0.0, jnp.where(ii > jj, top, unit))
        fh, fl = split(jnp.where(ii <= jj, top, 0.0))
        house = jnp.concatenate(
            [lower, gat[tick, k, pl.ds(block, height - block), :],
             jnp.zeros((SHIFT, block), f32)], 0)
        house = pltpu.roll(house, in_block(tick, k), 0)
        high, low = split(house)
        wide = dot(jnp.concatenate([high, low], 1), jnp.concatenate([fh, fh], 0))
        wh, wl = split(wide + dot(high, fl))
        wcat[slot, :, pl.ds(0, block)] = wh
        wcat[slot, :, pl.ds(block, block)] = wl
        ah, al = split(house.T)
        vhi[slot] = ah
        vlo[slot] = al

    def prepare_share(tick, owner):
        @pl.loop(0, per, unroll=1)
        def _(i):
            prepare(tick, owner * per + i)

    def apply(tick, k):
        slot = tick * n_dia + k
        window = pl.ds(pl.multiple_of(k * block, block), reach)
        vh, vl, wc = vhi[slot], vlo[slot], wcat[slot]
        slab = work[window, :]
        sh, sl = split(slab)
        hb = block // 2
        proj = jnp.concatenate([
            dot(vh[p:p + hb], sh) + (dot(vl[p:p + hb], sh) + dot(vh[p:p + hb], sl))
            for p in (0, hb)], 0)
        ph, plow = split(proj)
        pp = jnp.concatenate([ph, ph], 0)
        hr = reach // 2
        for p in (0, hr):
            part = wc[p:p + hr]
            delta = dot(part, pp) + dot(part[:, :block], plow)
            work[pl.ds(pl.multiple_of(k * block, block) + p, hr), :] = slab[p:p + hr] - delta

    def send_up(tick, c):
        part = pl.ds(c * chunk, chunk)
        return pltpu.make_async_remote_copy(
            src_ref=outb.at[tick, part], dst_ref=inflow.at[tick, part],
            send_sem=i_send.at[tick, c], recv_sem=i_recv.at[tick, c],
            device_id={"rows": above}, device_id_type=MESH)

    def send_down(tick):
        return pltpu.make_async_remote_copy(
            src_ref=tailb.at[tick], dst_ref=head.at[tick],
            send_sem=h_send.at[tick], recv_sem=h_recv.at[tick],
            device_id={"rows": below}, device_id_type=MESH)

    def take_head(tick):
        send_down(tick).wait_recv()
        work[pl.ds(0, block), left] = head[tick]

    @pl.loop(0, 2 * ticks)
    def _(m):
        mine = m < ticks
        tick = jnp.where(mine, m, m - ticks)

        @pl.when(mine)
        def _():
            own_copy(tick).wait()

        @pl.when(jnp.logical_not(mine))
        def _():
            to_partner(tick).wait_recv()

        prepare_share(tick, jnp.where(mine, col, partner))

    vec_copy.wait()

    @pl.loop(0, ticks)
    def _(tick):
        @pl.loop(0, n_dia)
        def _(counter):
            k = n_dia - 1 - counter
            owner, i = lax.div(k, per), lax.rem(k, per)
            o_chip, o_core = lax.div(owner, 2), lax.rem(owner, 2)
            j = lax.rem(chip + chips - o_chip, chips)

            @pl.when(j > 0)
            def _():
                def relay(at):
                    to_peer(tick, j, at).wait_recv()
                    forward(tick, j, at).start()

                @pl.when(jnp.logical_and(o_core == 1, i == per - 1))
                def _():
                    relay(i)

                @pl.when(o_core != core)
                def _():
                    forward(tick, j, i).wait_recv()

                prepare(tick, k)

                @pl.when(jnp.logical_and(o_core == 1, i > 0))
                def _():
                    relay(i - 1)

            @pl.when(jnp.logical_and(k == 0, jnp.logical_and(row > 0, tick > 0)))
            def _():
                take_head(jnp.maximum(tick - 1, 0))

            apply(tick, k)

        outb[tick] = work[pl.ds(0, block), left].T

        @pl.when(row == n_rows - 1)
        def _():
            for c in range(CHUNKS):
                send_up(tick, c).start()

        @pl.when(row < n_rows - 1)
        def _():
            mh, ml = split(work[pl.ds(0, block), right].T)
            for c in range(CHUNKS):
                send_up(tick, c).wait_recv()

                @pl.when(row > 0)
                def _():
                    part = pl.ds(c * chunk, chunk)
                    xh, xl = split(inflow[tick, part, :])
                    outb[tick, part, :] = outb[tick, part, :] + (
                        dot(xh, mh) + (dot(xl, mh) + dot(xh, ml)))
                    send_up(tick, c).start()

            flow = inflow[tick].T
            tail = pl.ds(rows_here, block)
            tailb[tick] = work[tail, left] + product(work[tail, right], flow)
            send_down(tick).start()
            fh, fl = split(flow)
            fcat = jnp.concatenate([fh, fh], 0)

            @pl.loop(0, rows_here // 256)
            def _(i):
                rows = pl.ds(pl.multiple_of(i * 256, 256), 256)
                rh, rl = split(work[rows, right])
                work[rows, left] = work[rows, left] + (
                    dot(jnp.concatenate([rh, rl], 1), fcat) + dot(rh, fl))

        @pl.when(tick < ticks - 1)
        def _():
            @pl.loop(0, rows_here // block)
            def _(i):
                work[pl.ds(pl.multiple_of(i * block, block), block), right] = zero
            reset()

    @pl.when(row > 0)
    def _():
        take_head(ticks - 1)

    out_copy = pltpu.make_async_copy(
        work.at[pl.ds(0, rows_here), pl.ds(0, width)], out_ref, vec_sem)
    out_copy.start()

    @pl.loop(0, ticks)
    def _(tick):
        @pl.loop(0, per)
        def _(i):
            for j in range(1, chips):
                to_peer(tick, j, i).wait_send()
                forward(tick, j, i).wait_send()
        to_partner(tick).wait_send()

        @pl.when(row > 0)
        def _():
            for c in range(CHUNKS):
                send_up(tick, c).wait_send()

        @pl.when(row < n_rows - 1)
        def _():
            send_down(tick).wait_send()

    out_copy.wait()


def solution(mesh):
    n_rows, n_cols = mesh.shape["rows"], mesh.shape["cols"]

    def on_device(vectors, reflectors, factors, starts):
        rows_here, width = vectors.shape
        ticks, per, height, block = reflectors.shape
        chips = n_cols // 2
        ii = lax.broadcasted_iota(jnp.int32, factors.shape, 2)
        jj = lax.broadcasted_iota(jnp.int32, factors.shape, 3)
        top = jnp.where(ii > jj, reflectors[:, :, :block], factors)
        packed = jnp.concatenate([top, reflectors[:, :, block:]], 2)
        dma = pltpu.SemaphoreType.DMA
        hops = max(chips - 1, 1)
        reach = height + SHIFT
        edge, flow = (ticks, block, width), (ticks, width, block)
        return pl.pallas_call(
            functools.partial(kernel, n_rows, n_cols),
            out_shape=jax.ShapeDtypeStruct(vectors.shape, f32),
            in_specs=[
                pl.BlockSpec(memory_space=pltpu.MemorySpace.HBM),
                pl.BlockSpec(memory_space=pl.ANY),
                pl.BlockSpec(memory_space=pltpu.SMEM),
            ],
            out_specs=pl.BlockSpec(memory_space=pl.ANY),
            scratch_shapes=[
                pltpu.VMEM((ticks, per * n_cols, height, block), f32),
                pltpu.VMEM((rows_here + height - block + SHIFT, width + block), f32),
                pltpu.VMEM((ticks * per * n_cols, block, reach), bf16),
                pltpu.VMEM((ticks * per * n_cols, block, reach), bf16),
                pltpu.VMEM((ticks * per * n_cols, reach, 2 * block), bf16),
                pltpu.VMEM(flow, f32), pltpu.VMEM(edge, f32),
                pltpu.VMEM(flow, f32), pltpu.VMEM(edge, f32),
                dma, dma((ticks,)),
                dma((ticks, hops, per)), dma((ticks, hops, per)),
                dma((ticks,)), dma((ticks,)),
                dma((ticks, hops, per)), dma((ticks, hops, per)),
                dma((ticks, CHUNKS)), dma((ticks, CHUNKS)), dma((ticks,)), dma((ticks,)),
            ],
            compiler_params=pltpu.CompilerParams(
                collective_id=0, has_side_effects=True, vmem_limit_bytes=36 * 2**20),
        )(vectors, packed, starts)

    return jax.shard_map(
        on_device,
        mesh=mesh,
        in_specs=(
            P("rows", "cols"),
            P(None, ("rows", "cols"), None, None),
            P(None, ("rows", "cols"), None, None),
            P(None, "rows"),
        ),
        out_specs=P("rows", "cols"),
        check_vma=False,
    )
```
